32 devices in a mesh: grp: 8 (over z, core), dev: 4 (over y, x).
Axes of the slice: x: 2, y: 2, z: 4, core: 2. Of those that a mesh axis runs over, the one named last changes fastest.
Arguments:
- sketch: float32 [32768, 512], P(('grp', 'dev')), may hold values from -50 to 50
- row_counts: int32 [32], P(('grp', 'dev')), may hold values from 0 to 1024, as said below
Outputs:
- q_factor: float32 [32768, 512], P(('grp', 'dev'))
- r_factor: float32 [512, 512], P('dev')
The draws below stay inside these ranges and needn't reach their ends.
Inputs may be any that keep to these rules, and one draw needn't show every extreme that they name: `row_counts`: every entry is a multiple of 128. Each aligned group of 4 consecutive entries sums to 1024, and in each such group at least one entry equals 1024.
All inputs are finite; a program needn't handle non-finite values.
Results may differ from the reference program's by a relative error of at most 0.00015.
Values sent between devices are 32-bit elements; how exact they have to be, the bound alone decides.
A program may use at most 128 MiB of HBM per device.

```python
import math
import jax
import jax.numpy as jnp
from jax import lax

W = 512
BLOCK = 64
SLOTS = 16
HOLD = 4
CAP = 1024
ROWS = 32768
USED = 8192
N_GRP = 8
N_DEV = 4
DEVICES = 32


def units_of_group(group_key):
    units_max = SLOTS // 2
    units_total = N_DEV * HOLD // 2
    key_heavy, key_order = jax.random.split(group_key)
    heavy = jax.random.randint(key_heavy, (), 0, N_DEV)
    ordering = jax.random.permutation(key_order, (N_DEV - 1) * units_max)
    chosen = ordering[:units_total - units_max] // units_max
    others = jnp.sum((chosen[:, None] == jnp.arange(N_DEV - 1)[None, :]).astype(jnp.int32), axis=0)
    members = jnp.arange(N_DEV)
    other_place = jnp.clip(members - (members > heavy).astype(jnp.int32), 0, N_DEV - 2)
    return jnp.where(members == heavy, units_max, others[other_place])


def draw_row_counts(key, part):
    group_keys = jax.random.split(jax.random.fold_in(key, 11), N_GRP)
    units = jax.vmap(units_of_group)(group_keys).reshape(-1)
    return (units * (2 * BLOCK)).astype(jnp.int32)


def pair_columns(values, pair_key, lowest, highest):
    key_order, key_weight = jax.random.split(pair_key)
    ordering = jax.random.permutation(key_order, W)
    pair_count = W // 8
    leading = ordering[:pair_count]
    trailing = ordering[pair_count:2 * pair_count]
    weights = jnp.exp(jax.random.uniform(key_weight, (pair_count,), jnp.float32, math.log(lowest), math.log(highest)))
    nearby = values[:, leading] + weights[None, :] * values[:, trailing]
    return values.at[:, trailing].set(nearby)


def device_rise(rise):
    place = (jnp.arange(ROWS, dtype=jnp.int32) // CAP).astype(jnp.float32) / max(DEVICES - 1, 1)
    return jnp.exp(math.log(rise) * place)[:, None]


def draw_sketch(key, part):
    keys = jax.random.split(jax.random.fold_in(key, 23), 6)
    values = jax.random.truncated_normal(keys[0], -6.0, 6.0, (ROWS, W), jnp.float32)
    return (device_rise(3.0) * pair_columns(values, keys[5], 0.2, 0.5)).astype(jnp.float32)


def setup_inputs(seed: int = 0) -> dict:
    streams_of = jax.random.split(jax.random.key(seed), 3)
    return {
        "sketch": draw_sketch(jax.random.fold_in(streams_of[2], 71), 0),
        "row_counts": draw_row_counts(jax.random.fold_in(streams_of[2], 71), 0),
    }


def reference(sketch, row_counts):
    shaped = sketch.reshape(DEVICES, SLOTS * BLOCK, W)
    inside = jnp.arange(SLOTS * BLOCK, dtype=jnp.int32)[None, :] < row_counts[:, None]
    masked = jnp.where(inside[:, :, None], shaped, jnp.zeros((), sketch.dtype)).reshape(-1, W)
    gram_sum = lax.dot_general(masked, masked, (((0,), (0,)), ((), ())), precision=lax.Precision.HIGHEST) / USED
    upper_factor = jnp.linalg.cholesky(gram_sum).T
    orthonormal = lax.linalg.triangular_solve(upper_factor, masked, left_side=False, lower=False)
    return (orthonormal, upper_factor)
```

```python
import functools

import jax
import jax.numpy as jnp
from jax import lax
from jax.experimental import pallas as pl
from jax.experimental.pallas import tpu as pltpu
from jax.sharding import PartitionSpec as P

SLOTS = 16
HOLD = 4
CORES = 2
TILE = 128
SUB = 8
VMEM_LIMIT = 60000 * 1024


def dot(left, right, left_dim, right_dim):
    return lax.dot_general(
        left,
        right,
        (((left_dim,), (right_dim,)), ((), ())),
        precision=lax.Precision.HIGHEST,
        preferred_element_type=jnp.float32,
    )


def upper_blocks(order):
    return [(i, j) for i in range(order) for j in range(i, order)]


def live(rows_in, count):
    row = lax.broadcasted_iota(jnp.int32, rows_in.shape, 0)
    return jnp.where(row < count, rows_in, jnp.zeros((), rows_in.dtype))


def gram_kernel(members, chips, count_ref, a_ref, out_ref, own, core_in, half, dev_in, quarter, z_in, send_sem, recv_sem):
    grp = lax.axis_index("grp")
    dev = lax.axis_index("dev")
    core = lax.rem(grp, CORES)
    z = lax.div(grp, CORES)
    columns = a_ref.shape[1]
    order = columns // TILE
    chunk = out_ref.shape[3]

    def core_peer(j):
        return (z * CORES + lax.rem(core + j, CORES), dev)

    def dev_peer(j):
        return (grp, lax.rem(dev + j, members))

    def z_peer(j):
        return (lax.rem(z + j, chips) * CORES + core, dev)

    greet = (
        [core_peer(j) for j in range(1, CORES)]
        + [dev_peer(j) for j in range(1, members)]
        + [z_peer(j) for j in range(1, chips)]
    )
    barrier = pltpu.get_barrier_semaphore()
    for peer in greet:
        pl.semaphore_signal(barrier, inc=1, device_id=peer, device_id_type=pl.DeviceIdType.MESH)

    rows = live(a_ref[...], count_ref[0])
    half_columns = columns // 2
    top = dot(rows[:, :half_columns], rows, 0, 0)
    bottom = dot(rows[:, half_columns:], rows[:, half_columns:], 0, 0)
    flat = own.reshape(own.size // TILE, TILE)
    for place, (i, j) in enumerate(upper_blocks(order)):
        if i < order // 2:
            block = top[i * TILE : (i + 1) * TILE, j * TILE : (j + 1) * TILE]
        else:
            low = i - order // 2
            right = j - order // 2
            block = bottom[low * TILE : (low + 1) * TILE, right * TILE : (right + 1) * TILE]
        flat[place * TILE : (place + 1) * TILE, :] = block
    used = len(upper_blocks(order)) * TILE
    if flat.shape[0] > used:
        flat[used:, :] = jnp.zeros((flat.shape[0] - used, TILE), jnp.float32)

    pl.semaphore_wait(barrier, len(greet))

    def copy(number, src, dst, peer):
        return pltpu.make_async_remote_copy(
            src_ref=src,
            dst_ref=dst,
            send_sem=send_sem.at[number],
            recv_sem=recv_sem.at[number],
            device_id=peer,
            device_id_type=pl.DeviceIdType.MESH,
        )

    pending = []
    number = 0

    def scatter(number, size, index, peer_of, source, landing):
        copies = []
        for j in range(1, size):
            c = copy(number + j - 1, source.at[lax.rem(index + j, size)], landing.at[j - 1], peer_of(j))
            c.start()
            copies.append(c)
        for c in copies:
            c.wait_recv()
        pending.extend(copies)
        total = source[index]
        for j in range(1, size):
            total = total + landing[j - 1]
        return total

    def gather(number, size, index, peer_of, target):
        copies = []
        for j in range(1, size):
            c = copy(number + j - 1, target.at[index], target.at[index], peer_of(j))
            c.start()
            copies.append(c)
        for j in range(1, size):
            sender = target.at[lax.rem(index + size - j, size)]
            copy(number + j - 1, sender, sender, peer_of(j)).wait_recv()
        pending.extend(copies)

    half[...] = scatter(number, CORES, core, core_peer, own, core_in)
    number += CORES - 1
    quarter[...] = scatter(number, members, dev, dev_peer, half, dev_in)
    number += members - 1
    out_ref[core, dev, z] = scatter(number, chips, z, z_peer, quarter, z_in)
    number += chips - 1
    gather(number, chips, z, z_peer, out_ref.at[core, dev])
    number += chips - 1
    gather(number, members, dev, dev_peer, out_ref.at[core])
    number += members - 1
    gather(number, CORES, core, core_peer, out_ref)
    for c in pending:
        c.wait_send()


def summed_gram(members, chips, own_count, sketch):
    columns = sketch.shape[1]
    used = len(upper_blocks(columns // TILE)) * TILE
    parts = CORES * members * chips
    chunk = -(-used // (parts * SUB)) * SUB
    shape = (CORES, members, chips, chunk, TILE)
    total = 2 * (CORES + members + chips - 3)
    packed = pl.pallas_call(
        functools.partial(gram_kernel, members, chips),
        out_shape=jax.ShapeDtypeStruct(shape, jnp.float32),
        in_specs=[
            pl.BlockSpec(memory_space=pltpu.SMEM),
            pl.BlockSpec(memory_space=pltpu.VMEM),
        ],
        out_specs=pl.BlockSpec(memory_space=pltpu.VMEM),
        scratch_shapes=[
            pltpu.VMEM(shape, jnp.float32),
            pltpu.VMEM((CORES - 1,) + shape[1:], jnp.float32),
            pltpu.VMEM(shape[1:], jnp.float32),
            pltpu.VMEM((members - 1,) + shape[2:], jnp.float32),
            pltpu.VMEM(shape[2:], jnp.float32),
            pltpu.VMEM((chips - 1,) + shape[3:], jnp.float32),
            pltpu.SemaphoreType.DMA((total,)),
            pltpu.SemaphoreType.DMA((total,)),
        ],
        compiler_params=pltpu.CompilerParams(
            collective_id=0, has_side_effects=True, vmem_limit_bytes=VMEM_LIMIT
        ),
        name="gram",
    )(own_count, sketch)
    return packed.reshape(parts * chunk, TILE)


def eliminate(block):
    tiles = TILE // SUB
    sub = lax.broadcasted_iota(jnp.int32, (SUB, TILE), 0)
    lane = lax.broadcasted_iota(jnp.int32, (SUB, TILE), 1)
    left = [block[t * SUB : (t + 1) * SUB, :] for t in range(tiles)]
    right = [jnp.where(sub + t * SUB == lane, 1.0, 0.0).astype(jnp.float32) for t in range(tiles)]

    def spread_row(tile, k):
        return jnp.broadcast_to(tile[k : k + 1, :], (SUB, TILE))

    for p in range(tiles):
        column = [
            [jnp.broadcast_to(left[t][:, p * SUB + k : p * SUB + k + 1], (SUB, TILE)) for t in range(p, tiles)]
            for k in range(SUB)
        ]
        for k in range(SUB):
            pivot = spread_row(column[k][0], k)
            inverse = 1.0 / pivot
            factor = [column[k][t] * inverse for t in range(tiles - p)]
            factor[0] = jnp.where(sub > k, factor[0], 0.0)
            for later in range(k + 1, SUB):
                entry = spread_row(column[later][0], k)
                for t in range(tiles - p):
                    column[later][t] = column[later][t] - factor[t] * entry
            left_row = spread_row(left[p], k)
            right_row = spread_row(right[p], k)
            for t in range(tiles - p):
                left[p + t] = left[p + t] - factor[t] * left_row
                right[p + t] = right[p + t] - factor[t] * right_row
            diagonal = pivot if k == 0 else jnp.where(sub >= k, pivot, diagonal)
        root = lax.rsqrt(diagonal)
        root = root * (1.5 - 0.5 * diagonal * root * root)
        left[p] = jnp.where(lane >= sub + p * SUB, left[p] * root, 0.0)
        right[p] = jnp.where(lane <= sub + p * SUB, right[p] * root, 0.0)
    return (jnp.concatenate(left, axis=0), jnp.concatenate(right, axis=0))


def factor_kernel(scale, own_ref, a_ref, packed_ref, q_ref, r_ref, schur, upper, inverse):
    columns = a_ref.shape[1]
    order = columns // TILE
    share = r_ref.shape[0]
    upper[...] = jnp.zeros_like(upper)
    inverse[...] = jnp.zeros_like(inverse)
    for place, (i, j) in enumerate(upper_blocks(order)):
        schur[i * TILE : (i + 1) * TILE, j * TILE : (j + 1) * TILE] = (
            packed_ref[place * TILE : (place + 1) * TILE, :] * scale
        )

    @pl.loop(0, order)
    def _(b):
        here = pl.ds(pl.multiple_of(b * TILE, TILE), TILE)
        upper_here, inverse_here = eliminate(schur[here, here])
        upper[here, here] = upper_here
        inverse[here, here] = inverse_here
        for step in range(order):

            @pl.when(b == step)
            def _():
                first, rest = step * TILE, (step + 1) * TILE
                own_inverse = inverse[first:rest, first:rest]
                if step < order - 1:
                    row = dot(own_inverse, schur[first:rest, rest:], 1, 0)
                    upper[first:rest, rest:] = row
                    schur[rest:, rest:] = schur[rest:, rest:] - dot(row, row, 0, 0)
                if step > 0:
                    mixed = dot(upper[:first, first:rest], inverse[:first, :first], 0, 0)
                    inverse[first:rest, :first] = -dot(own_inverse, mixed, 1, 0)

    r_ref[...] = upper[pl.ds(pl.multiple_of(own_ref[1] * share, share), share), :]
    half_columns = columns // 2
    rows = live(a_ref[...], own_ref[0])
    q_ref[:, :half_columns] = dot(rows[:, :half_columns], inverse[:half_columns, :half_columns], 1, 1)
    q_ref[:, half_columns:] = dot(rows, inverse[half_columns:, :], 1, 1)


def factored(scale, share, own, sketch, packed):
    columns = sketch.shape[1]
    vmem = pl.BlockSpec(memory_space=pltpu.VMEM)
    return pl.pallas_call(
        functools.partial(factor_kernel, scale),
        out_shape=(
            jax.ShapeDtypeStruct(sketch.shape, jnp.float32),
            jax.ShapeDtypeStruct((share, columns), jnp.float32),
        ),
        in_specs=[pl.BlockSpec(memory_space=pltpu.SMEM), vmem, vmem],
        out_specs=(vmem, vmem),
        scratch_shapes=[pltpu.VMEM((columns, columns), jnp.float32)] * 3,
        compiler_params=pltpu.CompilerParams(vmem_limit_bytes=VMEM_LIMIT),
        name="factor",
    )(own, sketch, packed)


def solution(mesh):
    groups, members = mesh.shape["grp"], mesh.shape["dev"]
    chips = groups // CORES

    def shards(sketch, row_counts):
        capacity, columns = sketch.shape
        row_total = groups * members * HOLD * (capacity // SLOTS)
        own = jnp.concatenate([row_counts, lax.axis_index("dev").astype(jnp.int32)[None]])
        packed = summed_gram(members, chips, row_counts, sketch)
        return factored(1.0 / row_total, columns // members, own, sketch, packed)

    return jax.shard_map(
        shards,
        mesh=mesh,
        in_specs=(P(("grp", "dev"), None), P(("grp", "dev"))),
        out_specs=(P(("grp", "dev"), None), P("dev", None)),
        check_vma=False,
    )
```

```python
import functools

import jax
import jax.numpy as jnp
from jax import lax
from jax.experimental import pallas as pl
from jax.experimental.pallas import tpu as pltpu
from jax.sharding import PartitionSpec as P

SLOTS = 16
HOLD = 4
CORES = 2
TILE = 128
SUB = 8
VMEM_LIMIT = 60000 * 1024
PIECES = 4


def dot(left, right, left_dim, right_dim):
    return lax.dot_general(
        left,
        right,
        (((left_dim,), (right_dim,)), ((), ())),
        precision=lax.Precision.HIGHEST,
        preferred_element_type=jnp.float32,
    )


def dot3(left, right, left_dim, right_dim):
    def part(one, other):
        return lax.dot_general(
            one, other, (((left_dim,), (right_dim,)), ((), ())), preferred_element_type=jnp.float32
        )

    left_high, right_high = left.astype(jnp.bfloat16), right.astype(jnp.bfloat16)
    left_low = (left - left_high.astype(jnp.float32)).astype(jnp.bfloat16)
    right_low = (right - right_high.astype(jnp.float32)).astype(jnp.bfloat16)
    return part(left_high, right_high) + (part(left_high, right_low) + part(left_low, right_high))


def upper_blocks(order):
    half = order // 2
    corner = [(i, j) for i in range(half) for j in range(half, order)]
    ends = [(i, j) for low in (0, half) for i in range(low, low + half) for j in range(i, low + half)]
    return corner + ends


def live(rows_in, count):
    row = lax.broadcasted_iota(jnp.int32, rows_in.shape, 0)
    return jnp.where(row < count, rows_in, jnp.zeros((), rows_in.dtype))


def gram_kernel(members, chips, count_ref, a_ref, out_ref, own, core_in, half, dev_in, quarter, z_in, send_sem, recv_sem):
    grp = lax.axis_index("grp")
    dev = lax.axis_index("dev")
    core = lax.rem(grp, CORES)
    z = lax.div(grp, CORES)
    columns = a_ref.shape[1]
    order = columns // TILE
    streams = out_ref.shape[0]

    def core_peer(j):
        return (z * CORES + lax.rem(core + j, CORES), dev)

    def dev_peer(j):
        return (grp, lax.rem(dev + j, members))

    def z_peer(j):
        return (lax.rem(z + j, chips) * CORES + core, dev)

    greet = (
        [core_peer(j) for j in range(1, CORES)]
        + [dev_peer(j) for j in range(1, members)]
        + [z_peer(j) for j in range(1, chips)]
    )
    barrier = pltpu.get_barrier_semaphore()
    for peer in greet:
        pl.semaphore_signal(barrier, inc=1, device_id=peer, device_id_type=pl.DeviceIdType.MESH)

    def copy(stream, number, src, dst, peer):
        return pltpu.make_async_remote_copy(
            src_ref=src,
            dst_ref=dst,
            send_sem=send_sem.at[stream, number],
            recv_sem=recv_sem.at[stream, number],
            device_id=peer,
            device_id_type=pl.DeviceIdType.MESH,
        )

    pending = []

    def scatter(stream, number, size, index, peer_of, source, landing):
        copies = []
        for j in range(1, size):
            c = copy(stream, number + j - 1, source.at[lax.rem(index + j, size)], landing.at[j - 1], peer_of(j))
            c.start()
            copies.append(c)
        pending.extend(copies)
        return copies

    def collect(copies, index, source, landing):
        for c in copies:
            c.wait_recv()
        total = source[index]
        for j in range(len(copies)):
            total = total + landing[j]
        return total

    def gather(stream, number, size, index, peer_of, target):
        copies = []
        for j in range(1, size):
            c = copy(stream, number + j - 1, target.at[index], target.at[index], peer_of(j))
            c.start()
            pending.append(c)
            sender = target.at[lax.rem(index + size - j, size)]
            copies.append(copy(stream, number + j - 1, sender, sender, peer_of(j)))
        return copies

    def arrive(copies):
        for c in copies:
            c.wait_recv()

    rows = live(a_ref[...], count_ref[0])
    middle = columns // 2
    flat = own.reshape(own.size // TILE, TILE)
    per_stream = own.size // TILE // streams
    places = upper_blocks(order)
    used = len(places) * TILE
    if flat.shape[0] > used:
        flat[used:, :] = jnp.zeros((flat.shape[0] - used, TILE), jnp.float32)
    corner = (order // 2) * (order - order // 2)
    end = (len(places) - corner) // 2
    pieces = (
        (0, corner, 0, middle),
        (corner, corner + end, 0, 0),
        (corner + end, len(places), middle, middle),
    )
    sent = 0
    first = [None] * streams
    for start, stop, row_at, column_at in pieces:
        tile = dot(rows[:, row_at : row_at + middle], rows[:, column_at : column_at + middle], 0, 0)
        for place in range(start, stop):
            i, j = places[place]
            top, left = i * TILE - row_at, j * TILE - column_at
            flat[place * TILE : (place + 1) * TILE, :] = tile[top : top + TILE, left : left + TILE]
        if start == 0:
            pl.semaphore_wait(barrier, len(greet))
        while sent < streams and ((sent + 1) * per_stream <= stop * TILE or stop == len(places)):
            first[sent] = scatter(sent, 0, CORES, core, core_peer, own.at[sent], core_in.at[sent])
            sent += 1

    second, third, fourth, fifth, sixth = ([None] * streams for _ in range(5))
    number = CORES - 1
    for s in range(streams):
        half[s] = collect(first[s], core, own.at[s], core_in.at[s])
        second[s] = scatter(s, number, members, dev, dev_peer, half.at[s], dev_in.at[s])
    number += members - 1
    for s in range(streams):
        quarter[s] = collect(second[s], dev, half.at[s], dev_in.at[s])
        third[s] = scatter(s, number, chips, z, z_peer, quarter.at[s], z_in.at[s])
    number += chips - 1
    for s in range(streams):
        out_ref[s, core, dev, z] = collect(third[s], z, quarter.at[s], z_in.at[s])
        fourth[s] = gather(s, number, chips, z, z_peer, out_ref.at[s, core, dev])
    number += chips - 1
    for s in range(streams):
        arrive(fourth[s])
        fifth[s] = gather(s, number, members, dev, dev_peer, out_ref.at[s, core])
    number += members - 1
    for s in range(streams):
        arrive(fifth[s])
        sixth[s] = gather(s, number, CORES, core, core_peer, out_ref.at[s])
    for s in range(streams):
        arrive(sixth[s])
    for c in pending:
        c.wait_send()


def summed_gram(members, chips, own_count, sketch):
    columns = sketch.shape[1]
    used = len(upper_blocks(columns // TILE)) * TILE
    parts = CORES * members * chips
    streams = -(-used // (parts * SUB))
    inner = (CORES, members, chips, SUB, TILE)
    total = 2 * (CORES + members + chips - 3)
    packed = pl.pallas_call(
        functools.partial(gram_kernel, members, chips),
        out_shape=jax.ShapeDtypeStruct((streams,) + inner, jnp.float32),
        in_specs=[
            pl.BlockSpec(memory_space=pltpu.SMEM),
            pl.BlockSpec(memory_space=pltpu.VMEM),
        ],
        out_specs=pl.BlockSpec(memory_space=pltpu.VMEM),
        scratch_shapes=[
            pltpu.VMEM((streams,) + inner, jnp.float32),
            pltpu.VMEM((streams, CORES - 1) + inner[1:], jnp.float32),
            pltpu.VMEM((streams,) + inner[1:], jnp.float32),
            pltpu.VMEM((streams, members - 1) + inner[2:], jnp.float32),
            pltpu.VMEM((streams,) + inner[2:], jnp.float32),
            pltpu.VMEM((streams, chips - 1) + inner[3:], jnp.float32),
            pltpu.SemaphoreType.DMA((streams, total)),
            pltpu.SemaphoreType.DMA((streams, total)),
        ],
        compiler_params=pltpu.CompilerParams(
            collective_id=0, has_side_effects=True, vmem_limit_bytes=VMEM_LIMIT
        ),
        name="gram",
    )(own_count, sketch)
    return packed.reshape(streams * parts * SUB, TILE)


def eliminate(block):
    tiles = TILE // SUB
    sub = lax.broadcasted_iota(jnp.int32, (SUB, TILE), 0)
    lane = lax.broadcasted_iota(jnp.int32, (SUB, TILE), 1)
    left = [block[t * SUB : (t + 1) * SUB, :] for t in range(tiles)]
    right = [jnp.where(sub + t * SUB == lane, 1.0, 0.0).astype(jnp.float32) for t in range(tiles)]

    def spread_row(tile, k):
        return jnp.broadcast_to(tile[k : k + 1, :], (SUB, TILE))

    for p in range(tiles):
        column = [
            [jnp.broadcast_to(left[t][:, p * SUB + k : p * SUB + k + 1], (SUB, TILE)) for t in range(p, tiles)]
            for k in range(SUB)
        ]
        for k in range(SUB):
            pivot = spread_row(column[k][0], k)
            inverse = 1.0 / pivot
            factor = [column[k][t] * inverse for t in range(tiles - p)]
            factor[0] = jnp.where(sub > k, factor[0], 0.0)
            for later in range(k + 1, SUB):
                entry = spread_row(column[later][0], k)
                for t in range(tiles - p):
                    column[later][t] = column[later][t] - factor[t] * entry
            left_row = spread_row(left[p], k)
            right_row = spread_row(right[p], k)
            for t in range(tiles - p):
                left[p + t] = left[p + t] - factor[t] * left_row
                right[p + t] = right[p + t] - factor[t] * right_row
            diagonal = pivot if k == 0 else jnp.where(sub >= k, pivot, diagonal)
        root = lax.rsqrt(diagonal)
        root = root * (1.5 - 0.5 * diagonal * root * root)
        left[p] = jnp.where(lane >= sub + p * SUB, left[p] * root, 0.0)
        right[p] = jnp.where(lane <= sub + p * SUB, right[p] * root, 0.0)
    return (jnp.concatenate(left, axis=0), jnp.concatenate(right, axis=0))


def factor_kernel(scale, count_ref, a_hbm, packed_ref, q_hbm, r_ref, schur, upper, inverse, a_ref, q_ref, in_sem, out_sem):
    fetch = pltpu.make_async_copy(a_hbm, a_ref, in_sem)
    fetch.start()
    columns = a_ref.shape[1]
    order = columns // TILE
    share = r_ref.shape[0]
    upper[...] = jnp.zeros_like(upper)
    inverse[...] = jnp.zeros_like(inverse)
    for place, (i, j) in enumerate(upper_blocks(order)):
        schur[i * TILE : (i + 1) * TILE, j * TILE : (j + 1) * TILE] = (
            packed_ref[place * TILE : (place + 1) * TILE, :] * scale
        )

    @pl.loop(0, order)
    def _(b):
        here = pl.ds(pl.multiple_of(b * TILE, TILE), TILE)
        upper_here, inverse_here = eliminate(schur[here, here])
        upper[here, here] = upper_here
        inverse[here, here] = inverse_here
        for step in range(order):

            @pl.when(b == step)
            def _():
                first, rest = step * TILE, (step + 1) * TILE
                own_inverse = inverse[first:rest, first:rest]
                if step < order - 1:
                    row = dot(own_inverse, schur[first:rest, rest:], 1, 0)
                    upper[first:rest, rest:] = row
                    schur[rest:, rest:] = schur[rest:, rest:] - dot(row, row, 0, 0)
                if step > 0:
                    mixed = dot(upper[:first, first:rest], inverse[:first, :first], 0, 0)
                    inverse[first:rest, :first] = -dot(own_inverse, mixed, 1, 0)

    own = lax.axis_index("dev")
    r_ref[...] = upper[pl.ds(pl.multiple_of(own * share, share), share), :]
    half_columns = columns // 2
    fetch.wait()
    step_rows = a_ref.shape[0] // PIECES
    stores = []
    for piece in range(PIECES):
        at = pl.ds(piece * step_rows, step_rows)
        rows = live(a_ref[at, :], count_ref[0] - piece * step_rows)
        q_ref[at, :half_columns] = dot3(rows[:, :half_columns], inverse[:half_columns, :half_columns], 1, 1)
        q_ref[at, half_columns:] = dot3(rows, inverse[half_columns:, :], 1, 1)
        store = pltpu.make_async_copy(q_ref.at[at], q_hbm.at[at], out_sem.at[piece])
        store.start()
        stores.append(store)
    for store in stores:
        store.wait()


def factored(scale, share, own_count, sketch, packed):
    columns = sketch.shape[1]
    vmem = pl.BlockSpec(memory_space=pltpu.VMEM)
    return pl.pallas_call(
        functools.partial(factor_kernel, scale),
        out_shape=(
            jax.ShapeDtypeStruct(sketch.shape, jnp.float32),
            jax.ShapeDtypeStruct((share, columns), jnp.float32),
        ),
        in_specs=[pl.BlockSpec(memory_space=pltpu.SMEM), pl.BlockSpec(memory_space=pl.ANY), vmem],
        out_specs=(pl.BlockSpec(memory_space=pl.ANY), vmem),
        scratch_shapes=[pltpu.VMEM((columns, columns), jnp.float32)] * 3
        + [pltpu.VMEM(sketch.shape, jnp.float32)] * 2
        + [pltpu.SemaphoreType.DMA, pltpu.SemaphoreType.DMA((PIECES,))],
        compiler_params=pltpu.CompilerParams(vmem_limit_bytes=VMEM_LIMIT),
        name="factor",
    )(own_count, sketch, packed)


def solution(mesh):
    groups, members = mesh.shape["grp"], mesh.shape["dev"]
    chips = groups // CORES

    def shards(sketch, row_counts):
        capacity, columns = sketch.shape
        row_total = groups * members * HOLD * (capacity // SLOTS)
        packed = summed_gram(members, chips, row_counts, sketch)
        return factored(1.0 / row_total, columns // members, row_counts, sketch, packed)

    return jax.shard_map(
        shards,
        mesh=mesh,
        in_specs=(P(("grp", "dev"), None), P(("grp", "dev"))),
        out_specs=(P(("grp", "dev"), None), P("dev", None)),
        check_vma=False,
    )
```

```python
import functools

import jax
import jax.numpy as jnp
from jax import lax
from jax.experimental import pallas as pl
from jax.experimental.pallas import tpu as pltpu
from jax.sharding import PartitionSpec as P

SLOTS = 16
HOLD = 4
CORES = 2
TILE = 128
SUB = 8
VMEM_LIMIT = 60000 * 1024
PIECES = 4
PANEL = 8
WIDTH = 2


def dot(left, right, left_dim, right_dim):
    return lax.dot_general(
        left,
        right,
        (((left_dim,), (right_dim,)), ((), ())),
        precision=lax.Precision.HIGHEST,
        preferred_element_type=jnp.float32,
    )


def dot3(left, right, left_dim, right_dim):
    def part(one, other):
        return lax.dot_general(
            one, other, (((left_dim,), (right_dim,)), ((), ())), preferred_element_type=jnp.float32
        )

    left_high, right_high = left.astype(jnp.bfloat16), right.astype(jnp.bfloat16)
    left_low = (left - left_high.astype(jnp.float32)).astype(jnp.bfloat16)
    right_low = (right - right_high.astype(jnp.float32)).astype(jnp.bfloat16)
    return part(left_high, right_high) + (part(left_high, right_low) + part(left_low, right_high))


def upper_blocks(order):
    half = order // 2
    corner = [(i, j) for i in range(half) for j in range(half, order)]
    ends = [(i, j) for low in (0, half) for i in range(low, low + half) for j in range(i, low + half)]
    return corner + ends


def live(rows_in, count):
    row = lax.broadcasted_iota(jnp.int32, rows_in.shape, 0)
    return jnp.where(row < count, rows_in, jnp.zeros((), rows_in.dtype))


def gram_kernel(members, chips, count_ref, a_ref, out_ref, own, core_in, half, dev_in, quarter, z_in, send_sem, recv_sem):
    grp = lax.axis_index("grp")
    dev = lax.axis_index("dev")
    core = lax.rem(grp, CORES)
    z = lax.div(grp, CORES)
    columns = a_ref.shape[1]
    order = columns // TILE
    streams = out_ref.shape[0]

    def core_peer(j):
        return (z * CORES + lax.rem(core + j, CORES), dev)

    def dev_peer(j):
        return (grp, lax.rem(dev + j, members))

    def z_peer(j):
        return (lax.rem(z + j, chips) * CORES + core, dev)

    greet = (
        [core_peer(j) for j in range(1, CORES)]
        + [dev_peer(j) for j in range(1, members)]
        + [z_peer(j) for j in range(1, chips)]
    )
    barrier = pltpu.get_barrier_semaphore()
    for peer in greet:
        pl.semaphore_signal(barrier, inc=1, device_id=peer, device_id_type=pl.DeviceIdType.MESH)

    def copy(stream, number, src, dst, peer):
        return pltpu.make_async_remote_copy(
            src_ref=src,
            dst_ref=dst,
            send_sem=send_sem.at[stream, number],
            recv_sem=recv_sem.at[stream, number],
            device_id=peer,
            device_id_type=pl.DeviceIdType.MESH,
        )

    pending = []

    def scatter(stream, number, size, index, peer_of, source, landing):
        copies = []
        for j in range(1, size):
            c = copy(stream, number + j - 1, source.at[lax.rem(index + j, size)], landing.at[j - 1], peer_of(j))
            c.start()
            copies.append(c)
        pending.extend(copies)
        return copies

    def collect(copies, index, source, landing):
        for c in copies:
            c.wait_recv()
        total = source[index]
        for j in range(len(copies)):
            total = total + landing[j]
        return total

    def gather(stream, number, size, index, peer_of, target):
        copies = []
        for j in range(1, size):
            c = copy(stream, number + j - 1, target.at[index], target.at[index], peer_of(j))
            c.start()
            pending.append(c)
            sender = target.at[lax.rem(index + size - j, size)]
            copies.append(copy(stream, number + j - 1, sender, sender, peer_of(j)))
        return copies

    def arrive(copies):
        for c in copies:
            c.wait_recv()

    rows = live(a_ref[...], count_ref[0])
    middle = columns // 2
    flat = own.reshape(own.size // TILE, TILE)
    per_stream = own.size // TILE // streams
    places = upper_blocks(order)
    used = len(places) * TILE
    if flat.shape[0] > used:
        flat[used:, :] = jnp.zeros((flat.shape[0] - used, TILE), jnp.float32)
    corner = (order // 2) * (order - order // 2)
    end = (len(places) - corner) // 2
    pieces = (
        (0, corner, 0, middle),
        (corner, corner + end, 0, 0),
        (corner + end, len(places), middle, middle),
    )
    sent = 0
    first = [None] * streams
    for start, stop, row_at, column_at in pieces:
        tile = dot(rows[:, row_at : row_at + middle], rows[:, column_at : column_at + middle], 0, 0)
        for place in range(start, stop):
            i, j = places[place]
            top, left = i * TILE - row_at, j * TILE - column_at
            flat[place * TILE : (place + 1) * TILE, :] = tile[top : top + TILE, left : left + TILE]
        if start == 0:
            pl.semaphore_wait(barrier, len(greet))
        while sent < streams and ((sent + 1) * per_stream <= stop * TILE or stop == len(places)):
            first[sent] = scatter(sent, 0, CORES, core, core_peer, own.at[sent], core_in.at[sent])
            sent += 1

    second, third, fourth, fifth, sixth = ([None] * streams for _ in range(5))
    number = CORES - 1
    for s in range(streams):
        half[s] = collect(first[s], core, own.at[s], core_in.at[s])
        second[s] = scatter(s, number, members, dev, dev_peer, half.at[s], dev_in.at[s])
    number += members - 1
    for s in range(streams):
        quarter[s] = collect(second[s], dev, half.at[s], dev_in.at[s])
        third[s] = scatter(s, number, chips, z, z_peer, quarter.at[s], z_in.at[s])
    number += chips - 1
    for s in range(streams):
        out_ref[s, core, dev, z] = collect(third[s], z, quarter.at[s], z_in.at[s])
        fourth[s] = gather(s, number, chips, z, z_peer, out_ref.at[s, core, dev])
    number += chips - 1
    for s in range(streams):
        arrive(fourth[s])
        fifth[s] = gather(s, number, members, dev, dev_peer, out_ref.at[s, core])
    number += members - 1
    for s in range(streams):
        arrive(fifth[s])
        sixth[s] = gather(s, number, CORES, core, core_peer, out_ref.at[s])
    for s in range(streams):
        arrive(sixth[s])
    for c in pending:
        c.wait_send()


def summed_gram(members, chips, own_count, sketch):
    columns = sketch.shape[1]
    used = len(upper_blocks(columns // TILE)) * TILE
    parts = CORES * members * chips
    streams = -(-used // (parts * SUB))
    inner = (CORES, members, chips, SUB, TILE)
    total = 2 * (CORES + members + chips - 3)
    packed = pl.pallas_call(
        functools.partial(gram_kernel, members, chips),
        out_shape=jax.ShapeDtypeStruct((streams,) + inner, jnp.float32),
        in_specs=[
            pl.BlockSpec(memory_space=pltpu.SMEM),
            pl.BlockSpec(memory_space=pltpu.VMEM),
        ],
        out_specs=pl.BlockSpec(memory_space=pltpu.VMEM),
        scratch_shapes=[
            pltpu.VMEM((streams,) + inner, jnp.float32),
            pltpu.VMEM((streams, CORES - 1) + inner[1:], jnp.float32),
            pltpu.VMEM((streams,) + inner[1:], jnp.float32),
            pltpu.VMEM((streams, members - 1) + inner[2:], jnp.float32),
            pltpu.VMEM((streams,) + inner[2:], jnp.float32),
            pltpu.VMEM((streams, chips - 1) + inner[3:], jnp.float32),
            pltpu.SemaphoreType.DMA((streams, total)),
            pltpu.SemaphoreType.DMA((streams, total)),
        ],
        compiler_params=pltpu.CompilerParams(
            collective_id=0, has_side_effects=True, vmem_limit_bytes=VMEM_LIMIT
        ),
        name="gram",
    )(own_count, sketch)
    return packed.reshape(streams * parts * SUB, TILE)


def eliminate(block):
    tiles = TILE // SUB
    sub = lax.broadcasted_iota(jnp.int32, (SUB, TILE), 0)
    lane = lax.broadcasted_iota(jnp.int32, (SUB, TILE), 1)
    left = [block[t * SUB : (t + 1) * SUB, :] for t in range(tiles)]
    right = [jnp.where(sub + t * SUB == lane, 1.0, 0.0).astype(jnp.float32) for t in range(tiles)]

    def spread_row(tile, k):
        return jnp.broadcast_to(tile[k : k + 1, :], (SUB, TILE))

    def finish(p, stop):
        column = [
            [jnp.broadcast_to(left[t][:, p * SUB + k : p * SUB + k + 1], (SUB, TILE)) for t in range(p, stop)]
            for k in range(WIDTH * SUB)
        ]
        diagonal = [None] * WIDTH
        for k in range(WIDTH * SUB):
            at, row = k // SUB, k % SUB
            below = range(at, stop - p)
            pivot = spread_row(column[k][at], row)
            inverse = 1.0 / pivot
            factor = {t: column[k][t] * inverse for t in below}
            factor[at] = jnp.where(sub > row, factor[at], 0.0)
            for later in range(k + 1, WIDTH * SUB):
                entry = spread_row(column[later][at], row)
                for t in below:
                    column[later][t] = column[later][t] - factor[t] * entry
            left_row = spread_row(left[p + at], row)
            right_row = spread_row(right[p + at], row)
            for t in below:
                left[p + t] = left[p + t] - factor[t] * left_row
                right[p + t] = right[p + t] - factor[t] * right_row
            diagonal[at] = pivot if row == 0 else jnp.where(sub >= row, pivot, diagonal[at])
        for t in range(WIDTH):
            root = lax.rsqrt(diagonal[t])
            root = root * (1.5 - 0.5 * diagonal[t] * root * root)
            place = sub + (p + t) * SUB
            left[p + t] = jnp.where(lane >= place, left[p + t] * root, 0.0)
            right[p + t] = jnp.where(lane <= place, right[p + t] * root, 0.0)

    for begin in range(0, tiles, PANEL):
        stop = begin + PANEL
        for p in range(begin, stop, WIDTH):
            finish(p, stop)
        if stop < tiles:
            upper_rows = jnp.concatenate(left[begin:stop], axis=0)
            inverse_rows = jnp.concatenate(right[begin:stop], axis=0)
            done = dot(upper_rows, jnp.concatenate([upper_rows, inverse_rows], axis=1), 0, 0)
            for t in range(stop, tiles):
                left[t] = left[t] - done[t * SUB : (t + 1) * SUB, :TILE]
                right[t] = right[t] - done[t * SUB : (t + 1) * SUB, TILE:]
    return (jnp.concatenate(left, axis=0), jnp.concatenate(right, axis=0))


def factor_kernel(scale, count_ref, a_hbm, packed_ref, q_hbm, r_ref, schur, upper, inverse, a_ref, q_ref, in_sem, out_sem):
    fetch = pltpu.make_async_copy(a_hbm, a_ref, in_sem)
    fetch.start()
    columns = a_ref.shape[1]
    order = columns // TILE
    share = r_ref.shape[0]
    upper[...] = jnp.zeros_like(upper)
    inverse[...] = jnp.zeros_like(inverse)
    for place, (i, j) in enumerate(upper_blocks(order)):
        schur[i * TILE : (i + 1) * TILE, j * TILE : (j + 1) * TILE] = (
            packed_ref[place * TILE : (place + 1) * TILE, :] * scale
        )

    @pl.loop(0, order)
    def _(b):
        here = pl.ds(pl.multiple_of(b * TILE, TILE), TILE)
        upper_here, inverse_here = eliminate(schur[here, here])
        upper[here, here] = upper_here
        inverse[here, here] = inverse_here
        for step in range(order):

            @pl.when(b == step)
            def _():
                first, rest = step * TILE, (step + 1) * TILE
                own_inverse = inverse[first:rest, first:rest]
                if step < order - 1:
                    row = dot3(own_inverse, schur[first:rest, rest:], 1, 0)
                    upper[first:rest, rest:] = row
                    schur[rest:, rest:] = schur[rest:, rest:] - dot(row, row, 0, 0)
                if step > 0:
                    mixed = dot3(upper[:first, first:rest], inverse[:first, :first], 0, 0)
                    inverse[first:rest, :first] = -dot3(own_inverse, mixed, 1, 0)

    own = lax.axis_index("dev")
    r_ref[...] = upper[pl.ds(pl.multiple_of(own * share, share), share), :]
    half_columns = columns // 2
    fetch.wait()
    step_rows = a_ref.shape[0] // PIECES
    stores = []
    for piece in range(PIECES):
        at = pl.ds(piece * step_rows, step_rows)
        rows = live(a_ref[at, :], count_ref[0] - piece * step_rows)
        q_ref[at, :half_columns] = dot3(rows[:, :half_columns], inverse[:half_columns, :half_columns], 1, 1)
        q_ref[at, half_columns:] = dot3(rows, inverse[half_columns:, :], 1, 1)
        store = pltpu.make_async_copy(q_ref.at[at], q_hbm.at[at], out_sem.at[piece])
        store.start()
        stores.append(store)
    for store in stores:
        store.wait()


def factored(scale, share, own_count, sketch, packed):
    columns = sketch.shape[1]
    vmem = pl.BlockSpec(memory_space=pltpu.VMEM)
    return pl.pallas_call(
        functools.partial(factor_kernel, scale),
        out_shape=(
            jax.ShapeDtypeStruct(sketch.shape, jnp.float32),
            jax.ShapeDtypeStruct((share, columns), jnp.float32),
        ),
        in_specs=[pl.BlockSpec(memory_space=pltpu.SMEM), pl.BlockSpec(memory_space=pl.ANY), vmem],
        out_specs=(pl.BlockSpec(memory_space=pl.ANY), vmem),
        scratch_shapes=[pltpu.VMEM((columns, columns), jnp.float32)] * 3
        + [pltpu.VMEM(sketch.shape, jnp.float32)] * 2
        + [pltpu.SemaphoreType.DMA, pltpu.SemaphoreType.DMA((PIECES,))],
        compiler_params=pltpu.CompilerParams(vmem_limit_bytes=VMEM_LIMIT),
        name="factor",
    )(own_count, sketch, packed)


def solution(mesh):
    groups, members = mesh.shape["grp"], mesh.shape["dev"]
    chips = groups // CORES

    def shards(sketch, row_counts):
        capacity, columns = sketch.shape
        row_total = groups * members * HOLD * (capacity // SLOTS)
        packed = summed_gram(members, chips, row_counts, sketch)
        return factored(1.0 / row_total, columns // members, row_counts, sketch, packed)

    return jax.shard_map(
        shards,
        mesh=mesh,
        in_specs=(P(("grp", "dev"), None), P(("grp", "dev"))),
        out_specs=(P(("grp", "dev"), None), P("dev", None)),
        check_vma=False,
    )
```
